512 devices in a mesh: row: 32 (over z_lo, y, core), col: 16 (over x, z_hi).
Axes of the slice: x: 4, y: 4, z: 16 (z_hi: 4, z_lo: 4; z = z_hi * 4 + z_lo), core: 2. Of those that a mesh axis runs over, the one named last changes fastest.
Arguments:
- row_cells: int32 [3, 32768], P(None, 'row'), may hold values from 0 to 63
- col_cells: int32 [3, 131072], P(None, 'col'), may hold values from 0 to 63
- omega: float32 [16, 131072], P(None, 'col'), may hold values from -6 to 6
Outputs:
- basis: float32 [16, 32768], P(None, 'row')
- image: float32 [16, 131072], P(None, 'col')
- core: float32 [16, 16], replicated
The draws below stay inside these ranges and needn't reach their ends.
All inputs are finite; a program needn't handle non-finite values.
Results may differ from the reference program's by a relative error of at most 0.0001.
Values sent between devices are 32-bit elements; how exact they have to be, the bound alone decides.
No kernel may reach another device: no remote copies, remote signals or barrier semaphores. Data moves between devices by JAX's collectives and lax.ppermute only.
A program may use at most 64 MiB of HBM per device.

```python
import math
import jax
import jax.numpy as jnp
from jax import lax

RANK = 16
GRID = 64
ROWS = 32768
ORDER = 131072


def plant(array, rng, least, top_value):
    index_at = [jax.random.randint(jax.random.fold_in(rng, axis), (), 0, length) for axis, length in enumerate(array.shape)]
    longest = array.shape.index(max(array.shape))
    neighbour = index_at[:longest] + [(index_at[longest] + 1) % array.shape[longest]] + index_at[longest + 1:]
    return array.at[tuple(index_at)].set(least).at[tuple(neighbour)].set(top_value)


def level_of(key, extent, cuts, low, high):
    level, own = 1.0, jax.random.fold_in(key, 6)
    for position, blocks in cuts:
        draws = jnp.exp(jax.random.uniform(jax.random.fold_in(own, position), (blocks,), jnp.float32, low / len(cuts), high / len(cuts)))
        level = level * jnp.repeat(draws, extent[position] // blocks).reshape([-1 if axis == position else 1 for axis in range(len(extent))])
    return level


def noise(stream_key, extent, deviation, limit, cuts=(), dtype=jnp.bfloat16):
    factor_of = level_of(stream_key, extent, cuts, -0.22, 0.18) if cuts else 1.0
    values = jax.random.normal(stream_key, extent, jnp.float32) * deviation * factor_of
    return jnp.minimum(jnp.maximum(values, -limit), limit).astype(dtype)


def setup_inputs(seed: int = 0) -> dict:
    splits = jax.random.split(jax.random.key(seed), 4)
    return {
        "row_cells": plant(jax.random.randint(splits[0], (3, ROWS), 0, GRID), jax.random.fold_in(splits[0], 1), 0, GRID - 1).astype(jnp.int32),
        "col_cells": plant(jax.random.randint(splits[1], (3, ORDER), 0, GRID), jax.random.fold_in(splits[1], 1), 0, GRID - 1).astype(jnp.int32),
        "omega": noise(splits[2], (RANK, ORDER), 1.0, 6.0, ((1, 16),), jnp.float32),
    }


def kernel_tile(rows, cols):
    first = (rows[0][:, None] - cols[0][None, :]).astype(jnp.float32)
    total = first * first
    second = (rows[1][:, None] - cols[1][None, :]).astype(jnp.float32)
    total = total + second * second
    third = (rows[2][:, None] - cols[2][None, :]).astype(jnp.float32)
    total = total + third * third
    return 0.25 * jnp.exp(-jnp.sqrt(total) / 6.4)

def reference(row_cells, col_cells, omega):
    rows_total = row_cells.shape[1]
    order = col_cells.shape[1]
    rank = omega.shape[0]
    block = math.gcd(rows_total, 512)
    count = rows_total // block
    row_blocks = row_cells.reshape(3, count, block).transpose(1, 0, 2)

    def sketch_block(cells):
        tile = kernel_tile(cells, col_cells)
        return lax.dot_general(omega, tile, (((1,), (1,)), ((), ())), precision=lax.Precision.HIGHEST)
    parts = lax.map(sketch_block, row_blocks)
    sketch = parts.transpose(1, 0, 2).reshape(rank, rows_total)
    gram = jnp.dot(sketch, sketch.T, precision=lax.Precision.HIGHEST) / rows_total
    lower = jnp.linalg.cholesky(gram)
    basis = jax.scipy.linalg.solve_triangular(lower, sketch, lower=True)
    basis_blocks = basis.reshape(rank, count, block).transpose(1, 0, 2)

    def image_step(carry, pair):
        cells, left = pair
        tile = kernel_tile(cells, col_cells)
        return (carry + jnp.dot(left, tile, precision=lax.Precision.HIGHEST), None)
    image, _ = lax.scan(image_step, jnp.zeros((rank, order), jnp.float32), (row_blocks, basis_blocks))
    core = jnp.dot(image, image.T, precision=lax.Precision.HIGHEST) / order
    return (basis, image, core)
```

```python
import functools
import math

import jax
import jax.numpy as jnp
from jax import lax
from jax.experimental import pallas as pl
from jax.experimental.pallas import tpu as pltpu
from jax.sharding import Mesh
from jax.sharding import PartitionSpec as P

ROW = ("zl", "y", "c")
COL = ("x", "zh")
RATE = math.log2(math.e) / 6.4
F32 = jnp.float32
BF16 = jnp.bfloat16
HIGHEST = lax.Precision.HIGHEST
LANES = 128
NT = (((1,), (1,)), ((), ()))
TINY = pl.CostEstimate(flops=1, bytes_accessed=1, transcendentals=0)


def exchanged(blocks, axes):
    return lax.all_to_all(blocks, axes, split_axis=0, concat_axis=0, tiled=True)


def features(cells, of_rows):
    v = cells.astype(F32)
    norm = v[0:1] * v[0:1] + v[1:2] * v[1:2] + v[2:3] * v[2:3]
    high = jnp.floor(norm * (1.0 / 128.0)) * 128.0
    low = norm - high
    one = jnp.ones_like(norm)
    if of_rows:
        parts = [-2.0 * v, one, one, high, low, jnp.zeros_like(norm)]
    else:
        parts = [v, high, low, one, one, jnp.zeros_like(norm)]
    return jnp.concatenate(parts, 0)


def in_two(value):
    high = value.astype(BF16)
    return high, (value - high.astype(F32)).astype(BF16)


def sketch_kernel(step_rows, rows_ref, cols_ref, tests_ref, sketch_ref, high_ref, low_ref, total, row_features):
    step = pl.program_id(0)

    @pl.when(step == 0)
    def _():
        row_features[...] = features(rows_ref[...], True).T.astype(BF16)
        total[...] = jnp.zeros_like(total)

    col_features = features(cols_ref[...], False).astype(BF16)
    tests = jnp.concatenate(in_two(tests_ref[...]), 0)
    for start in range(0, total.shape[1], step_rows):
        here = slice(start, start + step_rows)
        squared = jnp.dot(row_features[here, :], col_features, preferred_element_type=F32)
        squared = jnp.maximum(squared, 1e-20)
        high, low = in_two(jnp.exp2((squared * -RATE) * lax.rsqrt(squared)))
        high_ref[here, :] = high
        low_ref[here, :] = low
        total[:, here] += lax.dot_general(
            tests, high, NT, preferred_element_type=F32
        ) + lax.dot_general(tests, low, NT, preferred_element_type=F32)

    @pl.when(step == pl.num_programs(0) - 1)
    def _():
        rank = total.shape[0] // 2
        part = (total[:rank, :] + total[rank:, :]) * 0.25
        quarter = sketch_ref.shape[2]
        for peer in range(sketch_ref.shape[0]):
            sketch_ref[peer] = part[:, peer * quarter : (peer + 1) * quarter]


def sketch_call(row_cells, col_cells, omega, peers, width, step_rows):
    rank, cols = omega.shape
    rows = row_cells.shape[1]
    return pl.pallas_call(
        functools.partial(sketch_kernel, step_rows),
        grid=(cols // width,),
        in_specs=[
            pl.BlockSpec((3, rows), lambda i: (0, 0)),
            pl.BlockSpec((3, width), lambda i: (0, i)),
            pl.BlockSpec((rank, width), lambda i: (0, i)),
        ],
        out_specs=[
            pl.BlockSpec((peers, rank, rows // peers), lambda i: (0, 0, 0)),
            pl.BlockSpec((rows, width), lambda i: (0, i)),
            pl.BlockSpec((rows, width), lambda i: (0, i)),
            pl.BlockSpec((2 * rank, rows), lambda i: (0, 0)),
        ],
        out_shape=[
            jax.ShapeDtypeStruct((peers, rank, rows // peers), F32),
            jax.ShapeDtypeStruct((rows, cols), BF16),
            jax.ShapeDtypeStruct((rows, cols), BF16),
            jax.ShapeDtypeStruct((2 * rank, rows), F32),
        ],
        scratch_shapes=[pltpu.VMEM((rows, 8), BF16)],
        compiler_params=pltpu.CompilerParams(vmem_limit_bytes=62 << 20),
        name="sketch",
    )(row_cells, col_cells, omega)[:3]


def resend_kernel(arrived_ref, sent_ref):
    total = jnp.sum(arrived_ref[...], axis=0)
    for copy in range(sent_ref.shape[0]):
        sent_ref[copy] = total


def resend_call(arrived, copies, name):
    return pl.pallas_call(
        resend_kernel,
        out_shape=jax.ShapeDtypeStruct((copies, *arrived.shape[1:]), F32),
        cost_estimate=TINY,
        name=name,
    )(arrived)


def packed(square):
    half = square.shape[0] // 2
    rest = jnp.zeros((half, LANES - square.shape[1] * 2), F32)
    return jnp.concatenate([square[:half], square[half:], rest], 1)


def unpacked(tile, rank):
    return jnp.concatenate([tile[:, :rank], tile[:, rank : 2 * rank]], 0)


def image_kernel(share, arrived_ref, high_ref, low_ref, parts_ref, sketch_ref, left, gram):
    rank = arrived_ref.shape[1]

    @pl.when(pl.program_id(0) == 0)
    def _():
        sketch = jnp.concatenate([arrived_ref[peer] for peer in range(arrived_ref.shape[0])], 1)
        sketch_ref[...] = sketch
        left[...] = jnp.concatenate(in_two(sketch * 0.25), 0)
        gram[...] = packed(
            lax.dot_general(sketch, sketch, NT, precision=HIGHEST, preferred_element_type=F32)
        )

    product = jnp.dot(left[...], high_ref[...], preferred_element_type=F32) + jnp.dot(
        left[...], low_ref[...], preferred_element_type=F32
    )
    product = product[:rank] + product[rank:]
    pieces = share // LANES
    for block in range(parts_ref.shape[0]):
        for piece in range(pieces):
            at = block * share + piece * LANES
            parts_ref[block, piece * rank : (piece + 1) * rank, :] = product[:, at : at + LANES]
        parts_ref[block, pieces * rank :, :] = gram[...]


def image_call(arrived, high, low, peers, width):
    senders, rank, quarter = arrived.shape
    rows, cols = high.shape
    share = cols // peers
    height = share // LANES * rank + 8
    return pl.pallas_call(
        functools.partial(image_kernel, share),
        grid=(cols // width,),
        in_specs=[
            pl.BlockSpec((senders, rank, quarter), lambda i: (0, 0, 0)),
            pl.BlockSpec((rows, width), lambda i: (0, i)),
            pl.BlockSpec((rows, width), lambda i: (0, i)),
        ],
        out_specs=[
            pl.BlockSpec((width // share, height, LANES), lambda i: (i, 0, 0)),
            pl.BlockSpec((rank, rows), lambda i: (0, 0)),
        ],
        out_shape=[
            jax.ShapeDtypeStruct((peers, height, LANES), F32),
            jax.ShapeDtypeStruct((rank, rows), F32),
        ],
        scratch_shapes=[pltpu.VMEM((2 * rank, rows), BF16), pltpu.VMEM((8, LANES), F32)],
        compiler_params=pltpu.CompilerParams(vmem_limit_bytes=48 << 20),
        name="image",
    )(arrived, high, low)


def inverse_factor(gram):
    rank = gram.shape[0]
    row = lax.broadcasted_iota(jnp.int32, (rank, 1), 0)
    eye = (
        lax.broadcasted_iota(jnp.int32, (rank, rank), 0)
        == lax.broadcasted_iota(jnp.int32, (rank, rank), 1)
    ).astype(F32)
    state = jnp.concatenate([gram, eye, jnp.zeros((rank, LANES - 2 * rank), F32)], 1)
    for k in range(rank):
        scale = lax.rsqrt(state[k : k + 1, k : k + 1])
        pivot = state[k : k + 1, :] * scale
        column = state[:, k : k + 1] * scale
        below = state - column * pivot
        state = jnp.where(row > k, below, jnp.where(row == k, pivot, state))
    return state[:, rank : 2 * rank]


def factor_kernel(rows_total, arrived_ref, sketch_ref, share_ref, basis_ref):
    total = jnp.sum(arrived_ref[...], axis=0)
    rank = sketch_ref.shape[0]
    height = total.shape[0] - 8
    inverse = inverse_factor(unpacked(total[height:], rank) * (1.0 / rows_total))
    for piece in range(0, height, rank):
        part = jnp.dot(
            inverse, total[piece : piece + rank], precision=HIGHEST, preferred_element_type=F32
        )
        for copy in range(share_ref.shape[0]):
            share_ref[copy, piece : piece + rank, :] = part
    basis_ref[...] = jnp.dot(
        inverse, sketch_ref[...], precision=HIGHEST, preferred_element_type=F32
    )


def factor_call(arrived, sketch, rows_total):
    peers, height, _ = arrived.shape
    return pl.pallas_call(
        functools.partial(factor_kernel, rows_total),
        out_shape=[
            jax.ShapeDtypeStruct((peers, height - 8, LANES), F32),
            jax.ShapeDtypeStruct(sketch.shape, F32),
        ],
        name="factor",
    )(arrived, sketch)


def core_kernel(order, arrived_ref, core_ref):
    total = jnp.sum(arrived_ref[...], axis=0)
    core_ref[...] = unpacked(total, core_ref.shape[0]) * (1.0 / order)


def core_call(arrived, rank, order):
    return pl.pallas_call(
        functools.partial(core_kernel, order),
        out_shape=jax.ShapeDtypeStruct((rank, rank), F32),
        cost_estimate=TINY,
        name="core",
    )(arrived)


def joined_kernel(arrived_ref, image_ref, core_ref):
    rank = image_ref.shape[0]
    height = arrived_ref.shape[1]
    at = 0
    for peer in range(arrived_ref.shape[0]):
        for piece in range(0, height, rank):
            image_ref[:, at : at + LANES] = arrived_ref[peer, piece : piece + rank, :]
            at += LANES
    image = image_ref[...]
    tile = packed(
        lax.dot_general(image, image, NT, precision=HIGHEST, preferred_element_type=F32)
    )
    for copy in range(core_ref.shape[0]):
        core_ref[copy] = tile


def joined_call(arrived, rank, copies):
    peers, height, _ = arrived.shape
    return pl.pallas_call(
        joined_kernel,
        out_shape=[
            jax.ShapeDtypeStruct((rank, peers * height // rank * LANES), F32),
            jax.ShapeDtypeStruct((copies, 8, LANES), F32),
        ],
        name="joined",
    )(arrived)


def shards(row_cells, col_cells, omega):
    rank = omega.shape[0]
    local_rows = row_cells.shape[1]
    local_cols = col_cells.shape[1]
    rows_total = local_rows * lax.axis_size(ROW)
    order = local_cols * lax.axis_size(COL)
    peers = lax.axis_size("x")
    parts, high, low = sketch_call(row_cells, col_cells, omega, peers, 1024, 256)
    over_x = resend_call(exchanged(parts, "x"), lax.axis_size("zh"), "over_x")
    over_both = resend_call(exchanged(over_x, "zh"), peers, "over_zh")
    image_parts, sketch = image_call(exchanged(over_both, "x"), high, low, lax.axis_size(ROW), 2048)
    shares, basis = factor_call(exchanged(image_parts, ROW), sketch, rows_total)
    image, core_parts = joined_call(exchanged(shares, ROW), rank, lax.axis_size(COL))
    core = core_call(exchanged(core_parts, COL), rank, order)
    return (basis, image, core)


def solution(mesh):
    finer = Mesh(mesh.devices.reshape(4, 4, 2, 4, 4), ROW + COL)
    return jax.shard_map(
        shards,
        mesh=finer,
        in_specs=(P(None, ROW), P(None, COL), P(None, COL)),
        out_specs=(P(None, ROW), P(None, COL), P()),
        check_vma=False,
    )
```

```python
import functools
import math

import jax
import jax.numpy as jnp
from jax import lax
from jax.experimental import pallas as pl
from jax.experimental.pallas import tpu as pltpu
from jax.sharding import Mesh
from jax.sharding import PartitionSpec as P

ROW = ("zl", "y", "c")
COL = ("x", "zh")
RATE = math.log2(math.e) / 6.4
F32 = jnp.float32
BF16 = jnp.bfloat16
HIGHEST = lax.Precision.HIGHEST
LANES = 128
NT = (((1,), (1,)), ((), ()))
VMEM = pl.BlockSpec(memory_space=pltpu.VMEM)
SMALL = pltpu.CompilerParams(vmem_limit_bytes=8 << 20)


def exchanged(blocks, axes):
    return lax.all_to_all(blocks, axes, split_axis=0, concat_axis=0, tiled=True)


def features(cells, of_rows):
    v = cells.astype(F32)
    norm = v[0:1] * v[0:1] + v[1:2] * v[1:2] + v[2:3] * v[2:3]
    high = jnp.floor(norm * (1.0 / 128.0)) * 128.0
    low = norm - high
    one = jnp.ones_like(norm)
    if of_rows:
        parts = [-2.0 * v, one, one, high, low, jnp.zeros_like(norm)]
    else:
        parts = [v, high, low, one, one, jnp.zeros_like(norm)]
    return jnp.concatenate(parts, 0)


def in_two(value):
    high = value.astype(BF16)
    return high, (value - high.astype(F32)).astype(BF16)


def sketch_kernel(rows_ref, cols_ref, tests_ref, sketch_ref, matrix_ref, total, row_features):
    step = pl.program_id(0)

    @pl.when(step == 0)
    def _():
        row_features[...] = features(rows_ref[...], True).T.astype(BF16)
        total[...] = jnp.zeros_like(total)

    col_features = features(cols_ref[...], False).astype(BF16)
    tests = jnp.concatenate(in_two(tests_ref[...]), 0)
    blocks, _, _, width = matrix_ref.shape

    def evaluated(block):
        here = slice(block * width, (block + 1) * width)
        squared = jnp.dot(row_features[...], col_features[:, here], preferred_element_type=F32)
        squared = jnp.maximum(squared, 1e-20)
        high, low = in_two(jnp.exp2((squared * -RATE) * lax.rsqrt(squared)))
        matrix_ref[block, 0] = high
        matrix_ref[block, 1] = low
        return tests[:, here], high, low

    def summed(left, high, low):
        total[...] += lax.dot_general(
            left, high, NT, preferred_element_type=F32
        ) + lax.dot_general(left, low, NT, preferred_element_type=F32)

    waiting = evaluated(0)
    for block in range(1, blocks):
        latest = evaluated(block)
        summed(*waiting)
        waiting = latest
    summed(*waiting)

    @pl.when(step == pl.num_programs(0) - 1)
    def _():
        rank = total.shape[0] // 2
        part = (total[:rank, :] + total[rank:, :]) * 0.25
        quarter = sketch_ref.shape[2]
        for peer in range(sketch_ref.shape[0]):
            sketch_ref[peer] = part[:, peer * quarter : (peer + 1) * quarter]


def sketch_call(row_cells, col_cells, omega, peers, blocks, together):
    rank, cols = omega.shape
    rows = row_cells.shape[1]
    width = cols // blocks
    return pl.pallas_call(
        sketch_kernel,
        grid=(blocks // together,),
        in_specs=[
            pl.BlockSpec((3, rows), lambda i: (0, 0)),
            pl.BlockSpec((3, together * width), lambda i: (0, i)),
            pl.BlockSpec((rank, together * width), lambda i: (0, i)),
        ],
        out_specs=[
            pl.BlockSpec((peers, rank, rows // peers), lambda i: (0, 0, 0)),
            pl.BlockSpec((together, 2, rows, width), lambda i: (i, 0, 0, 0)),
            pl.BlockSpec((2 * rank, rows), lambda i: (0, 0)),
        ],
        out_shape=[
            jax.ShapeDtypeStruct((peers, rank, rows // peers), F32),
            jax.ShapeDtypeStruct((blocks, 2, rows, width), BF16),
            jax.ShapeDtypeStruct((2 * rank, rows), F32),
        ],
        scratch_shapes=[pltpu.VMEM((rows, 8), BF16)],
        compiler_params=pltpu.CompilerParams(vmem_limit_bytes=62 << 20),
        name="sketch",
    )(row_cells, col_cells, omega)[:2]


def resend_kernel(arrived_ref, sent_ref):
    total = jnp.sum(arrived_ref[...], axis=0)
    for copy in range(sent_ref.shape[0]):
        sent_ref[copy] = total


def resend_call(arrived, copies, name):
    return pl.pallas_call(
        resend_kernel,
        in_specs=[VMEM],
        out_specs=VMEM,
        out_shape=jax.ShapeDtypeStruct((copies, *arrived.shape[1:]), F32),
        compiler_params=SMALL,
        name=name,
    )(arrived)


def packed(square):
    half = square.shape[0] // 2
    rest = jnp.zeros((half, LANES - square.shape[1] * 2), F32)
    return jnp.concatenate([square[:half], square[half:], rest], 1)


def unpacked(tile, rank):
    return jnp.concatenate([tile[:, :rank], tile[:, rank : 2 * rank]], 0)


def image_kernel(together, arrived_ref, matrix_hbm, parts_ref, sketch_ref, matrix, arrivals):
    blocks, _, _, width = matrix.shape

    def copy_of(block):
        return pltpu.make_async_copy(
            matrix_hbm.at[block], matrix.at[block], arrivals.at[block]
        )

    for block in range(blocks):
        copy_of(block).start()
    senders, rank, _ = arrived_ref.shape
    sketch = jnp.concatenate([arrived_ref[peer] for peer in range(senders)], 1)
    sketch_ref[...] = sketch
    left = jnp.concatenate(in_two(sketch * 0.25), 0)
    gram = packed(
        lax.dot_general(sketch, sketch, NT, precision=HIGHEST, preferred_element_type=F32)
    )

    def step(index, carry):
        for offset in range(together):
            copy_of(index * together + offset).wait()
        for offset in range(together):
            block = index * together + offset
            product = jnp.dot(
                left, matrix[block, 0], preferred_element_type=F32
            ) + jnp.dot(left, matrix[block, 1], preferred_element_type=F32)
            product = product[:rank] + product[rank:]
            for piece in range(width // LANES):
                parts_ref[block, piece * rank : (piece + 1) * rank, :] = product[
                    :, piece * LANES : (piece + 1) * LANES
                ]
            parts_ref[block, width // LANES * rank :, :] = gram
        return carry

    lax.fori_loop(0, blocks // together, step, 0)


def image_call(arrived, matrix, together):
    senders, rank, quarter = arrived.shape
    blocks, _, rows, width = matrix.shape
    height = width // LANES * rank + 8
    return pl.pallas_call(
        functools.partial(image_kernel, together),
        in_specs=[VMEM, pl.BlockSpec(memory_space=pl.ANY)],
        out_specs=[VMEM, VMEM],
        out_shape=[
            jax.ShapeDtypeStruct((blocks, height, LANES), F32),
            jax.ShapeDtypeStruct((rank, rows), F32),
        ],
        scratch_shapes=[
            pltpu.VMEM(matrix.shape, BF16),
            pltpu.SemaphoreType.DMA((blocks,)),
        ],
        compiler_params=pltpu.CompilerParams(vmem_limit_bytes=48 << 20),
        name="image",
    )(arrived, matrix)


def inverse_factor(gram):
    rank = gram.shape[0]
    row = lax.broadcasted_iota(jnp.int32, (rank, 1), 0)
    eye = (
        lax.broadcasted_iota(jnp.int32, (rank, rank), 0)
        == lax.broadcasted_iota(jnp.int32, (rank, rank), 1)
    ).astype(F32)
    state = jnp.concatenate([gram, eye, jnp.zeros((rank, LANES - 2 * rank), F32)], 1)
    for k in range(rank):
        scale = lax.rsqrt(state[k : k + 1, k : k + 1])
        pivot = state[k : k + 1, :] * scale
        column = state[:, k : k + 1] * scale
        below = state - column * pivot
        state = jnp.where(row > k, below, jnp.where(row == k, pivot, state))
    return state[:, rank : 2 * rank]


def factor_kernel(rows_total, arrived_ref, sketch_ref, share_ref, basis_ref):
    total = jnp.sum(arrived_ref[...], axis=0)
    rank = sketch_ref.shape[0]
    height = total.shape[0] - 8
    inverse = inverse_factor(unpacked(total[height:], rank) * (1.0 / rows_total))
    for piece in range(0, height, rank):
        part = jnp.dot(
            inverse, total[piece : piece + rank], precision=HIGHEST, preferred_element_type=F32
        )
        for copy in range(share_ref.shape[0]):
            share_ref[copy, piece : piece + rank, :] = part
    basis_ref[...] = jnp.dot(
        inverse, sketch_ref[...], precision=HIGHEST, preferred_element_type=F32
    )


def factor_call(arrived, sketch, rows_total):
    peers, height, _ = arrived.shape
    return pl.pallas_call(
        functools.partial(factor_kernel, rows_total),
        in_specs=[VMEM, VMEM],
        out_specs=[VMEM, VMEM],
        out_shape=[
            jax.ShapeDtypeStruct((peers, height - 8, LANES), F32),
            jax.ShapeDtypeStruct(sketch.shape, F32),
        ],
        compiler_params=SMALL,
        name="factor",
    )(arrived, sketch)


def core_kernel(order, arrived_ref, core_ref):
    total = jnp.sum(arrived_ref[...], axis=0)
    core_ref[...] = unpacked(total, core_ref.shape[0]) * (1.0 / order)


def core_call(arrived, rank, order):
    return pl.pallas_call(
        functools.partial(core_kernel, order),
        in_specs=[VMEM],
        out_specs=VMEM,
        out_shape=jax.ShapeDtypeStruct((rank, rank), F32),
        compiler_params=SMALL,
        name="core",
    )(arrived)


def joined_kernel(arrived_ref, image_ref, core_ref):
    rank = image_ref.shape[0]
    height = arrived_ref.shape[1]
    at = 0
    for peer in range(arrived_ref.shape[0]):
        for piece in range(0, height, rank):
            image_ref[:, at : at + LANES] = arrived_ref[peer, piece : piece + rank, :]
            at += LANES
    image = image_ref[...]
    tile = packed(
        lax.dot_general(image, image, NT, precision=HIGHEST, preferred_element_type=F32)
    )
    for copy in range(core_ref.shape[0]):
        core_ref[copy] = tile


def joined_call(arrived, rank, copies):
    peers, height, _ = arrived.shape
    return pl.pallas_call(
        joined_kernel,
        in_specs=[VMEM],
        out_specs=[VMEM, VMEM],
        out_shape=[
            jax.ShapeDtypeStruct((rank, peers * height // rank * LANES), F32),
            jax.ShapeDtypeStruct((copies, 8, LANES), F32),
        ],
        compiler_params=SMALL,
        name="joined",
    )(arrived)


def shards(row_cells, col_cells, omega):
    rank = omega.shape[0]
    local_rows = row_cells.shape[1]
    local_cols = col_cells.shape[1]
    rows_total = local_rows * lax.axis_size(ROW)
    order = local_cols * lax.axis_size(COL)
    peers = lax.axis_size("x")
    parts, matrix = sketch_call(row_cells, col_cells, omega, peers, lax.axis_size(ROW), 4)
    over_x = resend_call(exchanged(parts, "x"), lax.axis_size("zh"), "over_x")
    over_both = resend_call(exchanged(over_x, "zh"), peers, "over_zh")
    image_parts, sketch = image_call(exchanged(over_both, "x"), matrix, 2)
    shares, basis = factor_call(exchanged(image_parts, ROW), sketch, rows_total)
    image, core_parts = joined_call(exchanged(shares, ROW), rank, lax.axis_size(COL))
    core = core_call(exchanged(core_parts, COL), rank, order)
    return (basis, image, core)


def solution(mesh):
    finer = Mesh(mesh.devices.reshape(4, 4, 2, 4, 4), ROW + COL)
    return jax.shard_map(
        shards,
        mesh=finer,
        in_specs=(P(None, ROW), P(None, COL), P(None, COL)),
        out_specs=(P(None, ROW), P(None, COL), P()),
        check_vma=False,
    )
```

```python
import functools
import math

import jax
import jax.numpy as jnp
from jax import lax
from jax.experimental import pallas as pl
from jax.experimental.pallas import tpu as pltpu
from jax.sharding import Mesh
from jax.sharding import PartitionSpec as P

ROW = ("zl", "y", "c")
COL = ("x", "zh")
RATE = math.log2(math.e) / 6.4
F32 = jnp.float32
BF16 = jnp.bfloat16
HIGHEST = lax.Precision.HIGHEST
LANES = 128
NT = (((1,), (1,)), ((), ()))
VMEM = pl.BlockSpec(memory_space=pltpu.VMEM)
SMALL = pltpu.CompilerParams(vmem_limit_bytes=8 << 20)


def exchanged(blocks, axes):
    return lax.all_to_all(blocks, axes, split_axis=0, concat_axis=0, tiled=True)


def swapped(block):
    return lax.ppermute(block, "c", [(0, 1), (1, 0)])


def features(cells, of_rows):
    v = cells.astype(F32)
    norm = v[0:1] * v[0:1] + v[1:2] * v[1:2] + v[2:3] * v[2:3]
    high = jnp.floor(norm * (1.0 / 128.0)) * 128.0
    low = norm - high
    one = jnp.ones_like(norm)
    if of_rows:
        parts = [-2.0 * v, one, one, high, low, jnp.zeros_like(norm)]
    else:
        parts = [v, high, low, one, one, jnp.zeros_like(norm)]
    return jnp.concatenate(parts, 0)


def in_two(value):
    high = value.astype(BF16)
    return high, (value - high.astype(F32)).astype(BF16)


def sketch_kernel(rows_ref, cols_ref, tests_ref, sketch_ref, matrix_ref, total, row_features):
    step = pl.program_id(0)

    @pl.when(step == 0)
    def _():
        row_features[...] = features(rows_ref[...], True).T.astype(BF16)
        total[...] = jnp.zeros_like(total)

    col_features = features(cols_ref[...], False).astype(BF16)
    tests = jnp.concatenate(in_two(tests_ref[...]), 0)
    blocks, _, _, width = matrix_ref.shape

    def evaluated(block):
        here = slice(block * width, (block + 1) * width)
        squared = jnp.dot(row_features[...], col_features[:, here], preferred_element_type=F32)
        squared = jnp.maximum(squared, 1e-20)
        high, low = in_two(jnp.exp2((squared * -RATE) * lax.rsqrt(squared)))
        matrix_ref[block, 0] = high
        matrix_ref[block, 1] = low
        return tests[:, here], high, low

    def summed(left, high, low):
        total[...] += lax.dot_general(
            left, high, NT, preferred_element_type=F32
        ) + lax.dot_general(left, low, NT, preferred_element_type=F32)

    waiting = evaluated(0)
    for block in range(1, blocks):
        latest = evaluated(block)
        summed(*waiting)
        waiting = latest
    summed(*waiting)

    @pl.when(step == pl.num_programs(0) - 1)
    def _():
        rank = total.shape[0] // 2
        part = (total[:rank, :] + total[rank:, :]) * 0.25
        quarter = sketch_ref.shape[2]
        for peer in range(sketch_ref.shape[0]):
            sketch_ref[peer] = part[:, peer * quarter : (peer + 1) * quarter]


def sketch_call(row_cells, col_cells, omega, peers, blocks, together):
    rank, cols = omega.shape
    rows = row_cells.shape[1]
    width = cols // blocks
    return pl.pallas_call(
        sketch_kernel,
        grid=(blocks // together,),
        in_specs=[
            pl.BlockSpec((3, rows), lambda i: (0, 0)),
            pl.BlockSpec((3, together * width), lambda i: (0, i)),
            pl.BlockSpec((rank, together * width), lambda i: (0, i)),
        ],
        out_specs=[
            pl.BlockSpec((peers, rank, rows // peers), lambda i: (0, 0, 0)),
            pl.BlockSpec((together, 2, rows, width), lambda i: (i, 0, 0, 0)),
            pl.BlockSpec((2 * rank, rows), lambda i: (0, 0)),
        ],
        out_shape=[
            jax.ShapeDtypeStruct((peers, rank, rows // peers), F32),
            jax.ShapeDtypeStruct((blocks, 2, rows, width), BF16),
            jax.ShapeDtypeStruct((2 * rank, rows), F32),
        ],
        scratch_shapes=[pltpu.VMEM((rows, 8), BF16)],
        compiler_params=pltpu.CompilerParams(vmem_limit_bytes=62 << 20),
        name="sketch",
    )(row_cells, col_cells, omega)[:2]


def resend_kernel(arrived_ref, sent_ref):
    total = jnp.sum(arrived_ref[...], axis=0)
    for copy in range(sent_ref.shape[0]):
        sent_ref[copy] = total


def resend_call(arrived, copies, name):
    return pl.pallas_call(
        resend_kernel,
        in_specs=[VMEM],
        out_specs=VMEM,
        out_shape=jax.ShapeDtypeStruct((copies, *arrived.shape[1:]), F32),
        compiler_params=SMALL,
        name=name,
    )(arrived)


def packed(square):
    half = square.shape[0] // 2
    rest = jnp.zeros((half, LANES - square.shape[1] * 2), F32)
    return jnp.concatenate([square[:half], square[half:], rest], 1)


def unpacked(tile, rank):
    return jnp.concatenate([tile[:, :rank], tile[:, rank : 2 * rank]], 0)


def image_blocks(together, core, left, gram, matrix_hbm, parts_ref, matrix, arrivals):
    blocks, _, _, width = matrix.shape
    rank = left.shape[0] // 2

    def copy_of(block):
        return pltpu.make_async_copy(
            matrix_hbm.at[2 * block + core], matrix.at[block], arrivals.at[block]
        )

    def step(index, carry):
        for offset in range(together):
            copy_of(index * together + offset).wait()
        for offset in range(together):
            block = index * together + offset
            product = jnp.dot(
                left[...], matrix[block, 0], preferred_element_type=F32
            ) + jnp.dot(left[...], matrix[block, 1], preferred_element_type=F32)
            product = product[:rank] + product[rank:]
            for piece in range(width // LANES):
                parts_ref[block, piece * rank : (piece + 1) * rank, :] = product[
                    :, piece * LANES : (piece + 1) * LANES
                ]
            parts_ref[block, width // LANES * rank :, :] = gram[...]
        return carry

    for block in range(blocks):
        copy_of(block).start()
    yield
    lax.fori_loop(0, blocks // together, step, 0)


def first_kernel(
    together, arrived_ref, matrix_hbm, parts_ref, sketch_ref, left_ref, gram_ref, matrix, arrivals
):
    core = 1 - lax.axis_index("c")
    work = image_blocks(
        together, core, left_ref, gram_ref, matrix_hbm, parts_ref, matrix, arrivals
    )
    next(work)
    senders = arrived_ref.shape[0]
    sketch = jnp.concatenate([arrived_ref[peer] for peer in range(senders)], 1)
    sketch_ref[...] = sketch
    left_ref[...] = jnp.concatenate(in_two(sketch * 0.25), 0)
    gram_ref[...] = packed(
        lax.dot_general(sketch, sketch, NT, precision=HIGHEST, preferred_element_type=F32)
    )
    for _ in work:
        pass


def second_kernel(together, left_ref, gram_ref, matrix_hbm, parts_ref, matrix, arrivals):
    core = lax.axis_index("c")
    for _ in image_blocks(
        together, core, left_ref, gram_ref, matrix_hbm, parts_ref, matrix, arrivals
    ):
        pass


def image_calls(arrived, matrix, together):
    senders, rank, quarter = arrived.shape
    blocks, _, rows, width = matrix.shape
    half = blocks // 2
    parts = jax.ShapeDtypeStruct((half, width // LANES * rank + 8, LANES), F32)
    options = {
        "scratch_shapes": [
            pltpu.VMEM((half, *matrix.shape[1:]), BF16),
            pltpu.SemaphoreType.DMA((half,)),
        ],
        "compiler_params": pltpu.CompilerParams(vmem_limit_bytes=32 << 20),
        "cost_estimate": pl.CostEstimate(
            flops=4 * rank * matrix.size, bytes_accessed=matrix.size, transcendentals=0
        ),
    }
    first, sketch, left, gram = pl.pallas_call(
        functools.partial(first_kernel, together),
        in_specs=[VMEM, pl.BlockSpec(memory_space=pl.ANY)],
        out_specs=[VMEM] * 4,
        out_shape=[
            parts,
            jax.ShapeDtypeStruct((rank, rows), F32),
            jax.ShapeDtypeStruct((2 * rank, rows), BF16),
            jax.ShapeDtypeStruct((8, LANES), F32),
        ],
        name="image_of_other",
        **options,
    )(arrived, matrix)
    second = pl.pallas_call(
        functools.partial(second_kernel, together),
        in_specs=[VMEM, VMEM, pl.BlockSpec(memory_space=pl.ANY)],
        out_specs=VMEM,
        out_shape=parts,
        name="image_of_own",
        **options,
    )(left, gram, matrix)
    return first, second, sketch


def pair_kernel(own_ref, other_ref, sum_ref):
    sum_ref[...] = own_ref[...] + other_ref[...]


def pair_call(own, other):
    return pl.pallas_call(
        pair_kernel,
        in_specs=[VMEM, VMEM],
        out_specs=VMEM,
        out_shape=jax.ShapeDtypeStruct(own.shape, F32),
        compiler_params=SMALL,
        name="pair",
    )(own, other)


def inverse_factor(gram):
    rank = gram.shape[0]
    row = lax.broadcasted_iota(jnp.int32, (rank, 1), 0)
    eye = (
        lax.broadcasted_iota(jnp.int32, (rank, rank), 0)
        == lax.broadcasted_iota(jnp.int32, (rank, rank), 1)
    ).astype(F32)
    state = jnp.concatenate([gram, eye, jnp.zeros((rank, LANES - 2 * rank), F32)], 1)
    for k in range(rank):
        scale = lax.rsqrt(state[k : k + 1, k : k + 1])
        pivot = state[k : k + 1, :] * scale
        column = state[:, k : k + 1] * scale
        below = state - column * pivot
        state = jnp.where(row > k, below, jnp.where(row == k, pivot, state))
    return state[:, rank : 2 * rank]


def factor_kernel(rows_total, arrived_ref, sketch_ref, share_ref, basis_ref):
    total = jnp.sum(arrived_ref[...], axis=0)
    rank = sketch_ref.shape[0]
    height = total.shape[0] - 8
    inverse = inverse_factor(unpacked(total[height:], rank) * (1.0 / rows_total))
    for piece in range(0, height, rank):
        part = jnp.dot(
            inverse, total[piece : piece + rank], precision=HIGHEST, preferred_element_type=F32
        )
        for copy in range(share_ref.shape[0]):
            share_ref[copy, piece : piece + rank, :] = part
    basis_ref[...] = jnp.dot(
        inverse, sketch_ref[...], precision=HIGHEST, preferred_element_type=F32
    )


def factor_call(arrived, sketch, rows_total):
    peers, height, _ = arrived.shape
    return pl.pallas_call(
        functools.partial(factor_kernel, rows_total),
        in_specs=[VMEM, VMEM],
        out_specs=[VMEM, VMEM],
        out_shape=[
            jax.ShapeDtypeStruct((peers, height - 8, LANES), F32),
            jax.ShapeDtypeStruct(sketch.shape, F32),
        ],
        compiler_params=SMALL,
        name="factor",
    )(arrived, sketch)


def core_kernel(order, arrived_ref, core_ref):
    total = jnp.sum(arrived_ref[...], axis=0)
    core_ref[...] = unpacked(total, core_ref.shape[0]) * (1.0 / order)


def core_call(arrived, rank, order):
    return pl.pallas_call(
        functools.partial(core_kernel, order),
        in_specs=[VMEM],
        out_specs=VMEM,
        out_shape=jax.ShapeDtypeStruct((rank, rank), F32),
        compiler_params=SMALL,
        name="core",
    )(arrived)


def square_kernel(arrived_ref, square_ref):
    senders, height, _ = arrived_ref.shape
    rank = height // 2
    pieces = [
        arrived_ref[sender, piece * rank : (piece + 1) * rank, :]
        for sender in range(senders)
        for piece in range(2)
    ]
    image = jnp.concatenate(pieces, 1)
    tile = packed(
        lax.dot_general(image, image, NT, precision=HIGHEST, preferred_element_type=F32)
    )
    for copy in range(square_ref.shape[0]):
        square_ref[copy] = tile


def square_call(arrived, copies):
    return pl.pallas_call(
        square_kernel,
        in_specs=[VMEM],
        out_specs=VMEM,
        out_shape=jax.ShapeDtypeStruct((copies, 8, LANES), F32),
        compiler_params=SMALL,
        name="square",
    )(arrived)


def joined_kernel(own_ref, other_ref, image_ref):
    core = lax.axis_index("c")
    rank = image_ref.shape[0]
    senders, height, _ = own_ref.shape
    pieces = height // rank
    for sender in range(senders):
        for ref, half in ((own_ref, core), (other_ref, 1 - core)):
            for piece in range(pieces):
                at = pl.multiple_of(((2 * sender + half) * pieces + piece) * LANES, LANES)
                image_ref[:, pl.ds(at, LANES)] = ref[sender, piece * rank : (piece + 1) * rank, :]


def joined_call(own, other, rank):
    senders, height, _ = own.shape
    return pl.pallas_call(
        joined_kernel,
        in_specs=[VMEM, VMEM],
        out_specs=VMEM,
        out_shape=jax.ShapeDtypeStruct((rank, 2 * senders * height // rank * LANES), F32),
        compiler_params=SMALL,
        name="joined",
    )(own, other)


def shards(row_cells, col_cells, omega):
    rank = omega.shape[0]
    local_rows = row_cells.shape[1]
    local_cols = col_cells.shape[1]
    rows_total = local_rows * lax.axis_size(ROW)
    order = local_cols * lax.axis_size(COL)
    peers = lax.axis_size("x")
    parts, matrix = sketch_call(row_cells, col_cells, omega, peers, lax.axis_size(ROW), 4)
    over_x = resend_call(exchanged(parts, "x"), lax.axis_size("zh"), "over_x")
    over_both = resend_call(exchanged(over_x, "zh"), peers, "over_zh")
    first, second, sketch = image_calls(exchanged(over_both, "x"), matrix, 2)
    chip_parts = pair_call(second, swapped(first))
    shares, basis = factor_call(exchanged(chip_parts, ("zl", "y")), sketch, rows_total)
    own = exchanged(shares, ("zl", "y"))
    other = swapped(own)
    square_parts = square_call(own, lax.axis_size(COL + ("c",)))
    core = core_call(exchanged(square_parts, COL + ("c",)), rank, order)
    image = joined_call(own, other, rank)
    return (basis, image, core)


def solution(mesh):
    finer = Mesh(mesh.devices.reshape(4, 4, 2, 4, 4), ROW + COL)
    return jax.shard_map(
        shards,
        mesh=finer,
        in_specs=(P(None, ROW), P(None, COL), P(None, COL)),
        out_specs=(P(None, ROW), P(None, COL), P()),
        check_vma=False,
    )
```

```python
import functools
import math

import jax
import jax.numpy as jnp
from jax import lax
from jax.experimental import pallas as pl
from jax.experimental.pallas import tpu as pltpu
from jax.sharding import Mesh
from jax.sharding import PartitionSpec as P

ROW = ("zl", "y", "c")
COL = ("x", "zh")
RATE = math.log2(math.e) / 6.4
F32 = jnp.float32
BF16 = jnp.bfloat16
HIGHEST = lax.Precision.HIGHEST
LANES = 128
NT = (((1,), (1,)), ((), ()))
VMEM = pl.BlockSpec(memory_space=pltpu.VMEM)
SMALL = pltpu.CompilerParams(vmem_limit_bytes=8 << 20)


def exchanged(blocks, axes):
    return lax.all_to_all(blocks, axes, split_axis=0, concat_axis=0, tiled=True)


def swapped(block):
    return lax.ppermute(block, "c", [(0, 1), (1, 0)])


def features(cells, of_rows):
    v = cells.astype(F32)
    norm = v[0:1] * v[0:1] + v[1:2] * v[1:2] + v[2:3] * v[2:3]
    high = jnp.floor(norm * (1.0 / 128.0)) * 128.0
    low = norm - high
    one = jnp.ones_like(norm)
    if of_rows:
        parts = [-2.0 * v, one, one, high, low, jnp.zeros_like(norm)]
    else:
        parts = [v, high, low, one, one, jnp.zeros_like(norm)]
    return jnp.concatenate(parts, 0)


def in_two(value):
    high = value.astype(BF16)
    return high, (value - high.astype(F32)).astype(BF16)


def sketch_kernel(rows_ref, cols_ref, tests_ref, sketch_ref, matrix_ref, total, row_features):
    step = pl.program_id(0)

    @pl.when(step == 0)
    def _():
        row_features[...] = features(rows_ref[...], True).T.astype(BF16)
        total[...] = jnp.zeros_like(total)

    col_features = features(cols_ref[...], False).astype(BF16)
    tests = jnp.concatenate(in_two(tests_ref[...]), 0)
    blocks, _, _, width = matrix_ref.shape

    def evaluated(block):
        here = slice(block * width, (block + 1) * width)
        squared = jnp.dot(row_features[...], col_features[:, here], preferred_element_type=F32)
        squared = jnp.maximum(squared, 1e-20)
        high, low = in_two(jnp.exp2((squared * -RATE) * lax.rsqrt(squared)))
        matrix_ref[block, 0] = high
        matrix_ref[block, 1] = low
        return tests[:, here], high, low

    def summed(left, high, low):
        total[...] += lax.dot_general(
            left, high, NT, preferred_element_type=F32
        ) + lax.dot_general(left, low, NT, preferred_element_type=F32)

    waiting = evaluated(0)
    for block in range(1, blocks):
        latest = evaluated(block)
        summed(*waiting)
        waiting = latest
    summed(*waiting)

    @pl.when(step == pl.num_programs(0) - 1)
    def _():
        rank = total.shape[0] // 2
        part = (total[:rank, :] + total[rank:, :]) * 0.25
        quarter = sketch_ref.shape[2]
        for peer in range(sketch_ref.shape[0]):
            sketch_ref[peer] = part[:, peer * quarter : (peer + 1) * quarter]


def sketch_call(row_cells, col_cells, omega, peers, blocks, together):
    rank, cols = omega.shape
    rows = row_cells.shape[1]
    width = cols // blocks
    return pl.pallas_call(
        sketch_kernel,
        grid=(blocks // together,),
        in_specs=[
            pl.BlockSpec((3, rows), lambda i: (0, 0)),
            pl.BlockSpec((3, together * width), lambda i: (0, i)),
            pl.BlockSpec((rank, together * width), lambda i: (0, i)),
        ],
        out_specs=[
            pl.BlockSpec((peers, rank, rows // peers), lambda i: (0, 0, 0)),
            pl.BlockSpec((together, 2, rows, width), lambda i: (i, 0, 0, 0)),
            pl.BlockSpec((2 * rank, rows), lambda i: (0, 0)),
        ],
        out_shape=[
            jax.ShapeDtypeStruct((peers, rank, rows // peers), F32),
            jax.ShapeDtypeStruct((blocks, 2, rows, width), BF16),
            jax.ShapeDtypeStruct((2 * rank, rows), F32),
        ],
        scratch_shapes=[pltpu.VMEM((rows, 8), BF16)],
        compiler_params=pltpu.CompilerParams(vmem_limit_bytes=62 << 20),
        name="sketch",
    )(row_cells, col_cells, omega)[:2]


def resend_kernel(arrived_ref, sent_ref):
    total = jnp.sum(arrived_ref[...], axis=0)
    for copy in range(sent_ref.shape[0]):
        sent_ref[copy] = total


def resend_call(arrived, copies, name):
    return pl.pallas_call(
        resend_kernel,
        in_specs=[VMEM],
        out_specs=VMEM,
        out_shape=jax.ShapeDtypeStruct((copies, *arrived.shape[1:]), F32),
        compiler_params=SMALL,
        name=name,
    )(arrived)


def packed(square):
    half = square.shape[0] // 2
    rest = jnp.zeros((half, LANES - square.shape[1] * 2), F32)
    return jnp.concatenate([square[:half], square[half:], rest], 1)


def unpacked(tile, rank):
    return jnp.concatenate([tile[:, :rank], tile[:, rank : 2 * rank]], 0)


def image_blocks(together, core, left, gram, matrix_hbm, parts_ref, matrix, arrivals):
    blocks, _, _, width = matrix.shape
    rank = left.shape[0] // 2

    def copy_of(block):
        return pltpu.make_async_copy(
            matrix_hbm.at[2 * block + core], matrix.at[block], arrivals.at[block]
        )

    def step(index, carry):
        for offset in range(together):
            copy_of(index * together + offset).wait()
        for offset in range(together):
            block = index * together + offset
            product = jnp.dot(
                left[...], matrix[block, 0], preferred_element_type=F32
            ) + jnp.dot(left[...], matrix[block, 1], preferred_element_type=F32)
            product = product[:rank] + product[rank:]
            for piece in range(width // LANES):
                parts_ref[block, piece * rank : (piece + 1) * rank, :] = product[
                    :, piece * LANES : (piece + 1) * LANES
                ]
            parts_ref[block, width // LANES * rank :, :] = gram[...]
        return carry

    for block in range(blocks):
        copy_of(block).start()
    yield
    lax.fori_loop(0, blocks // together, step, 0)


def first_kernel(
    together, arrived_ref, matrix_hbm, parts_ref, sketch_ref, left_ref, gram_ref, matrix, arrivals
):
    core = 1 - lax.axis_index("c")
    work = image_blocks(
        together, core, left_ref, gram_ref, matrix_hbm, parts_ref, matrix, arrivals
    )
    next(work)
    senders = arrived_ref.shape[0]
    sketch = jnp.concatenate([arrived_ref[peer] for peer in range(senders)], 1)
    sketch_ref[...] = sketch
    left_ref[...] = jnp.concatenate(in_two(sketch * 0.25), 0)
    gram_ref[...] = packed(
        lax.dot_general(sketch, sketch, NT, precision=HIGHEST, preferred_element_type=F32)
    )
    for _ in work:
        pass


def second_kernel(together, left_ref, gram_ref, matrix_hbm, parts_ref, matrix, arrivals):
    core = lax.axis_index("c")
    for _ in image_blocks(
        together, core, left_ref, gram_ref, matrix_hbm, parts_ref, matrix, arrivals
    ):
        pass


def image_calls(arrived, matrix, together):
    senders, rank, quarter = arrived.shape
    blocks, _, rows, width = matrix.shape
    half = blocks // 2
    parts = jax.ShapeDtypeStruct((half, width // LANES * rank + 8, LANES), F32)
    options = {
        "scratch_shapes": [
            pltpu.VMEM((half, *matrix.shape[1:]), BF16),
            pltpu.SemaphoreType.DMA((half,)),
        ],
        "compiler_params": pltpu.CompilerParams(vmem_limit_bytes=32 << 20),
        "cost_estimate": pl.CostEstimate(
            flops=4 * rank * matrix.size, bytes_accessed=matrix.size, transcendentals=0
        ),
    }
    first, sketch, left, gram = pl.pallas_call(
        functools.partial(first_kernel, together),
        in_specs=[VMEM, pl.BlockSpec(memory_space=pl.ANY)],
        out_specs=[VMEM] * 4,
        out_shape=[
            parts,
            jax.ShapeDtypeStruct((rank, rows), F32),
            jax.ShapeDtypeStruct((2 * rank, rows), BF16),
            jax.ShapeDtypeStruct((8, LANES), F32),
        ],
        name="image_of_other",
        **options,
    )(arrived, matrix)
    second = pl.pallas_call(
        functools.partial(second_kernel, together),
        in_specs=[VMEM, VMEM, pl.BlockSpec(memory_space=pl.ANY)],
        out_specs=VMEM,
        out_shape=parts,
        name="image_of_own",
        **options,
    )(left, gram, matrix)
    return first, second, sketch


def pair_kernel(own_ref, other_ref, sum_ref):
    sum_ref[...] = own_ref[...] + other_ref[...]


def pair_call(own, other):
    return pl.pallas_call(
        pair_kernel,
        in_specs=[VMEM, VMEM],
        out_specs=VMEM,
        out_shape=jax.ShapeDtypeStruct(own.shape, F32),
        compiler_params=SMALL,
        name="pair",
    )(own, other)


def inverse_factor(gram):
    rank = gram.shape[0]
    row = lax.broadcasted_iota(jnp.int32, (rank, 1), 0)
    eye = (
        lax.broadcasted_iota(jnp.int32, (rank, rank), 0)
        == lax.broadcasted_iota(jnp.int32, (rank, rank), 1)
    ).astype(F32)
    state = jnp.concatenate([gram, eye, jnp.zeros((rank, LANES - 2 * rank), F32)], 1)
    for k in range(rank):
        scale = lax.rsqrt(state[k : k + 1, k : k + 1])
        pivot = state[k : k + 1, :] * scale
        column = state[:, k : k + 1] * scale
        below = state - column * pivot
        state = jnp.where(row > k, below, jnp.where(row == k, pivot, state))
    return state[:, rank : 2 * rank]


def share_kernel(arrived_ref, share_ref, gram_ref):
    total = jnp.sum(arrived_ref[...], axis=0)
    height = share_ref.shape[1]
    for copy in range(share_ref.shape[0]):
        share_ref[copy] = total[:height]
    gram_ref[...] = total[height:]


def share_call(arrived):
    peers, height, _ = arrived.shape
    return pl.pallas_call(
        share_kernel,
        in_specs=[VMEM],
        out_specs=[VMEM, VMEM],
        out_shape=[
            jax.ShapeDtypeStruct((peers, height - 8, LANES), F32),
            jax.ShapeDtypeStruct((8, LANES), F32),
        ],
        compiler_params=SMALL,
        name="share",
    )(arrived)


def factor_kernel(rows_total, gram_ref, sketch_ref, inverse_ref, basis_ref):
    rank = sketch_ref.shape[0]
    inverse = inverse_factor(unpacked(gram_ref[...], rank) * (1.0 / rows_total))
    inverse_ref[...] = inverse
    basis_ref[...] = jnp.dot(
        inverse, sketch_ref[...], precision=HIGHEST, preferred_element_type=F32
    )


def factor_call(gram, sketch, rows_total):
    rank = sketch.shape[0]
    return pl.pallas_call(
        functools.partial(factor_kernel, rows_total),
        in_specs=[VMEM, VMEM],
        out_specs=[VMEM, VMEM],
        out_shape=[
            jax.ShapeDtypeStruct((rank, rank), F32),
            jax.ShapeDtypeStruct(sketch.shape, F32),
        ],
        compiler_params=SMALL,
        cost_estimate=pl.CostEstimate(
            flops=1 << 30, bytes_accessed=8 << 20, transcendentals=0
        ),
        name="factor",
    )(gram, sketch)


def core_kernel(order, arrived_ref, inverse_ref, core_ref):
    square = unpacked(jnp.sum(arrived_ref[...], axis=0), core_ref.shape[0]) * (1.0 / order)
    inverse = inverse_ref[...]
    half = jnp.dot(inverse, square, precision=HIGHEST, preferred_element_type=F32)
    core_ref[...] = lax.dot_general(
        half, inverse, NT, precision=HIGHEST, preferred_element_type=F32
    )


def core_call(arrived, inverse, order):
    return pl.pallas_call(
        functools.partial(core_kernel, order),
        in_specs=[VMEM, VMEM],
        out_specs=VMEM,
        out_shape=jax.ShapeDtypeStruct(inverse.shape, F32),
        compiler_params=SMALL,
        name="core",
    )(arrived, inverse)


def square_kernel(arrived_ref, square_ref):
    senders, height, _ = arrived_ref.shape
    rank = height // 2
    pieces = [
        arrived_ref[sender, piece * rank : (piece + 1) * rank, :]
        for sender in range(senders)
        for piece in range(2)
    ]
    image = jnp.concatenate(pieces, 1)
    tile = packed(
        lax.dot_general(image, image, NT, precision=HIGHEST, preferred_element_type=F32)
    )
    for copy in range(square_ref.shape[0]):
        square_ref[copy] = tile


def square_call(arrived, copies):
    return pl.pallas_call(
        square_kernel,
        in_specs=[VMEM],
        out_specs=VMEM,
        out_shape=jax.ShapeDtypeStruct((copies, 8, LANES), F32),
        compiler_params=SMALL,
        name="square",
    )(arrived)


def joined_kernel(own_ref, other_ref, inverse_ref, image_ref):
    core = lax.axis_index("c")
    rank = image_ref.shape[0]
    senders, height, _ = own_ref.shape
    pieces = height // rank
    span = pieces * LANES
    for ref, half in ((own_ref, core), (other_ref, 1 - core)):
        raw = jnp.concatenate(
            [
                ref[sender, piece * rank : (piece + 1) * rank, :]
                for sender in range(senders)
                for piece in range(pieces)
            ],
            1,
        )
        image = jnp.dot(
            inverse_ref[...], raw, precision=HIGHEST, preferred_element_type=F32
        )
        for sender in range(senders):
            at = pl.multiple_of((2 * sender + half) * span, LANES)
            image_ref[:, pl.ds(at, span)] = image[:, sender * span : (sender + 1) * span]


def joined_call(own, other, inverse):
    senders, height, _ = own.shape
    rank = inverse.shape[0]
    return pl.pallas_call(
        joined_kernel,
        in_specs=[VMEM, VMEM, VMEM],
        out_specs=VMEM,
        out_shape=jax.ShapeDtypeStruct((rank, 2 * senders * height // rank * LANES), F32),
        compiler_params=SMALL,
        name="joined",
    )(own, other, inverse)


def shards(row_cells, col_cells, omega):
    rank = omega.shape[0]
    local_rows = row_cells.shape[1]
    local_cols = col_cells.shape[1]
    rows_total = local_rows * lax.axis_size(ROW)
    order = local_cols * lax.axis_size(COL)
    peers = lax.axis_size("x")
    parts, matrix = sketch_call(row_cells, col_cells, omega, peers, lax.axis_size(ROW), 4)
    over_x = resend_call(exchanged(parts, "x"), lax.axis_size("zh"), "over_x")
    over_both = resend_call(exchanged(over_x, "zh"), peers, "over_zh")
    first, second, sketch = image_calls(exchanged(over_both, "x"), matrix, 2)
    chip_parts = pair_call(second, swapped(first))
    shares, gram = share_call(exchanged(chip_parts, ("zl", "y")))
    own = exchanged(shares, ("zl", "y"))
    inverse, basis = factor_call(gram, sketch, rows_total)
    other = swapped(own)
    square_parts = square_call(own, lax.axis_size(COL + ("c",)))
    core = core_call(exchanged(square_parts, COL + ("c",)), inverse, order)
    image = joined_call(own, other, inverse)
    return (basis, image, core)


def solution(mesh):
    finer = Mesh(mesh.devices.reshape(4, 4, 2, 4, 4), ROW + COL)
    return jax.shard_map(
        shards,
        mesh=finer,
        in_specs=(P(None, ROW), P(None, COL), P(None, COL)),
        out_specs=(P(None, ROW), P(None, COL), P()),
        check_vma=False,
    )
```

```python
import functools
import math

import jax
import jax.numpy as jnp
from jax import lax
from jax.experimental import pallas as pl
from jax.experimental.pallas import tpu as pltpu
from jax.sharding import Mesh
from jax.sharding import PartitionSpec as P

ROW = ("zl", "y", "c")
COL = ("x", "zh")
RATE = math.log2(math.e) / 6.4
F32 = jnp.float32
BF16 = jnp.bfloat16
HIGHEST = lax.Precision.HIGHEST
LANES = 128
NT = (((1,), (1,)), ((), ()))
VMEM = pl.BlockSpec(memory_space=pltpu.VMEM)
SMALL = pltpu.CompilerParams(vmem_limit_bytes=8 << 20)


def exchanged(blocks, axes):
    return lax.all_to_all(blocks, axes, split_axis=0, concat_axis=0, tiled=True)


def swapped(block):
    return lax.ppermute(block, "c", [(0, 1), (1, 0)])


def features(cells, of_rows):
    v = cells.astype(F32)
    norm = v[0:1] * v[0:1] + v[1:2] * v[1:2] + v[2:3] * v[2:3]
    high = jnp.floor(norm * (1.0 / 128.0)) * 128.0
    low = norm - high
    one = jnp.ones_like(norm)
    if of_rows:
        parts = [-2.0 * v, one, one, high, low, jnp.zeros_like(norm)]
    else:
        parts = [v, high, low, one, one, jnp.zeros_like(norm)]
    return jnp.concatenate(parts, 0)


def in_two(value):
    high = value.astype(BF16)
    return high, (value - high.astype(F32)).astype(BF16)


def sketch_kernel(rows_ref, cols_ref, tests_ref, sketch_ref, matrix_ref, total, row_features):
    step = pl.program_id(0)

    @pl.when(step == 0)
    def _():
        row_features[...] = features(rows_ref[...], True).T.astype(BF16)
        total[...] = jnp.zeros_like(total)

    col_features = features(cols_ref[...], False).astype(BF16)
    tests = jnp.concatenate(in_two(tests_ref[...]), 0)
    blocks, _, _, width = matrix_ref.shape

    def evaluated(block):
        here = slice(block * width, (block + 1) * width)
        squared = jnp.dot(row_features[...], col_features[:, here], preferred_element_type=F32)
        squared = jnp.maximum(squared, 1e-20)
        high, low = in_two(jnp.exp2((squared * -RATE) * lax.rsqrt(squared)))
        matrix_ref[block, 0] = high
        matrix_ref[block, 1] = low
        return tests[:, here], high, low

    def summed(left, high, low):
        total[...] += lax.dot_general(
            left, high, NT, preferred_element_type=F32
        ) + lax.dot_general(left, low, NT, preferred_element_type=F32)

    waiting = evaluated(0)
    for block in range(1, blocks):
        latest = evaluated(block)
        summed(*waiting)
        waiting = latest
    summed(*waiting)

    @pl.when(step == pl.num_programs(0) - 1)
    def _():
        rank = total.shape[0] // 2
        part = (total[:rank, :] + total[rank:, :]) * 0.25
        quarter = sketch_ref.shape[2]
        for peer in range(sketch_ref.shape[0]):
            sketch_ref[peer] = part[:, peer * quarter : (peer + 1) * quarter]


def sketch_call(row_cells, col_cells, omega, peers, blocks, together):
    rank, cols = omega.shape
    rows = row_cells.shape[1]
    width = cols // blocks
    return pl.pallas_call(
        sketch_kernel,
        grid=(blocks // together,),
        in_specs=[
            pl.BlockSpec((3, rows), lambda i: (0, 0)),
            pl.BlockSpec((3, together * width), lambda i: (0, i)),
            pl.BlockSpec((rank, together * width), lambda i: (0, i)),
        ],
        out_specs=[
            pl.BlockSpec((peers, rank, rows // peers), lambda i: (0, 0, 0)),
            pl.BlockSpec((together, 2, rows, width), lambda i: (i, 0, 0, 0)),
            pl.BlockSpec((2 * rank, rows), lambda i: (0, 0)),
        ],
        out_shape=[
            jax.ShapeDtypeStruct((peers, rank, rows // peers), F32),
            jax.ShapeDtypeStruct((blocks, 2, rows, width), BF16),
            jax.ShapeDtypeStruct((2 * rank, rows), F32),
        ],
        scratch_shapes=[pltpu.VMEM((rows, 8), BF16)],
        compiler_params=pltpu.CompilerParams(vmem_limit_bytes=62 << 20),
        name="sketch",
    )(row_cells, col_cells, omega)[:2]


def resend_kernel(arrived_ref, sent_ref):
    total = jnp.sum(arrived_ref[...], axis=0)
    for copy in range(sent_ref.shape[0]):
        sent_ref[copy] = total


def resend_call(arrived, copies, name):
    return pl.pallas_call(
        resend_kernel,
        in_specs=[VMEM],
        out_specs=VMEM,
        out_shape=jax.ShapeDtypeStruct((copies, *arrived.shape[1:]), F32),
        compiler_params=SMALL,
        name=name,
    )(arrived)


def packed(square):
    half = square.shape[0] // 2
    rest = jnp.zeros((half, LANES - square.shape[1] * 2), F32)
    return jnp.concatenate([square[:half], square[half:], rest], 1)


def unpacked(tile, rank):
    return jnp.concatenate([tile[:, :rank], tile[:, rank : 2 * rank]], 0)


def image_blocks(together, core, left, gram, matrix_hbm, parts_ref, matrix, arrivals):
    blocks, _, _, width = matrix.shape
    rank = left.shape[0] // 2

    def copy_of(block):
        return pltpu.make_async_copy(
            matrix_hbm.at[2 * block + core], matrix.at[block], arrivals.at[block]
        )

    def step(index, carry):
        for offset in range(together):
            copy_of(index * together + offset).wait()
        for offset in range(together):
            block = index * together + offset
            product = jnp.dot(
                left[...], matrix[block, 0], preferred_element_type=F32
            ) + jnp.dot(left[...], matrix[block, 1], preferred_element_type=F32)
            product = product[:rank] + product[rank:]
            for piece in range(width // LANES):
                parts_ref[block, piece * rank : (piece + 1) * rank, :] = product[
                    :, piece * LANES : (piece + 1) * LANES
                ]
            parts_ref[block, width // LANES * rank :, :] = gram[...]
        return carry

    for block in range(blocks):
        copy_of(block).start()
    yield
    lax.fori_loop(0, blocks // together, step, 0)


def first_kernel(
    together, arrived_ref, matrix_hbm, parts_ref, sketch_ref, left_ref, gram_ref, matrix, arrivals
):
    core = 1 - lax.axis_index("c")
    work = image_blocks(
        together, core, left_ref, gram_ref, matrix_hbm, parts_ref, matrix, arrivals
    )
    next(work)
    senders = arrived_ref.shape[0]
    sketch = jnp.concatenate([arrived_ref[peer] for peer in range(senders)], 1)
    sketch_ref[...] = sketch
    left_ref[...] = jnp.concatenate(in_two(sketch * 0.25), 0)
    gram_ref[...] = packed(
        lax.dot_general(sketch, sketch, NT, precision=HIGHEST, preferred_element_type=F32)
    )
    for _ in work:
        pass


def second_kernel(together, left_ref, gram_ref, matrix_hbm, parts_ref, matrix, arrivals):
    core = lax.axis_index("c")
    for _ in image_blocks(
        together, core, left_ref, gram_ref, matrix_hbm, parts_ref, matrix, arrivals
    ):
        pass


def image_calls(arrived, matrix, together):
    senders, rank, quarter = arrived.shape
    blocks, _, rows, width = matrix.shape
    half = blocks // 2
    parts = jax.ShapeDtypeStruct((half, width // LANES * rank + 8, LANES), F32)
    options = {
        "scratch_shapes": [
            pltpu.VMEM((half, *matrix.shape[1:]), BF16),
            pltpu.SemaphoreType.DMA((half,)),
        ],
        "compiler_params": pltpu.CompilerParams(vmem_limit_bytes=32 << 20),
        "cost_estimate": pl.CostEstimate(
            flops=4 * rank * matrix.size, bytes_accessed=matrix.size, transcendentals=0
        ),
    }
    first, sketch, left, gram = pl.pallas_call(
        functools.partial(first_kernel, together),
        in_specs=[VMEM, pl.BlockSpec(memory_space=pl.ANY)],
        out_specs=[VMEM] * 4,
        out_shape=[
            parts,
            jax.ShapeDtypeStruct((rank, rows), F32),
            jax.ShapeDtypeStruct((2 * rank, rows), BF16),
            jax.ShapeDtypeStruct((8, LANES), F32),
        ],
        name="image_of_other",
        **options,
    )(arrived, matrix)
    second = pl.pallas_call(
        functools.partial(second_kernel, together),
        in_specs=[VMEM, VMEM, pl.BlockSpec(memory_space=pl.ANY)],
        out_specs=VMEM,
        out_shape=parts,
        name="image_of_own",
        **options,
    )(left, gram, matrix)
    return first, second, sketch


def pair_kernel(own_ref, other_ref, sum_ref):
    sum_ref[...] = own_ref[...] + other_ref[...]


def pair_call(own, other):
    return pl.pallas_call(
        pair_kernel,
        in_specs=[VMEM, VMEM],
        out_specs=VMEM,
        out_shape=jax.ShapeDtypeStruct(own.shape, F32),
        compiler_params=SMALL,
        name="pair",
    )(own, other)


def inverse_factor(gram):
    rank = gram.shape[0]
    row = lax.broadcasted_iota(jnp.int32, (rank, 1), 0)
    eye = (
        lax.broadcasted_iota(jnp.int32, (rank, rank), 0)
        == lax.broadcasted_iota(jnp.int32, (rank, rank), 1)
    ).astype(F32)
    state = jnp.concatenate([gram, eye, jnp.zeros((rank, LANES - 2 * rank), F32)], 1)
    for k in range(rank):
        scale = lax.rsqrt(state[k : k + 1, k : k + 1])
        pivot = state[k : k + 1, :] * scale
        column = state[:, k : k + 1] * scale
        below = state - column * pivot
        state = jnp.where(row > k, below, jnp.where(row == k, pivot, state))
    return state[:, rank : 2 * rank]


def flattened(square):
    rank = square.shape[0]
    side = LANES // rank
    return jnp.concatenate(
        [
            jnp.concatenate([square[at + row : at + row + 1] for row in range(side)], 1)
            for at in range(0, rank, side)
        ],
        0,
    )


def restored(flat, rank):
    side = LANES // rank
    return jnp.concatenate(
        [
            flat[row // side : row // side + 1, row % side * rank : (row % side + 1) * rank]
            for row in range(rank)
        ],
        0,
    )


def share_kernel(arrived_ref, share_ref, gram_ref):
    total = jnp.sum(arrived_ref[...], axis=0)
    height = share_ref.shape[1]
    for copy in range(share_ref.shape[0]):
        share_ref[copy] = total[:height]
    gram_ref[...] = total[height:]


def share_call(arrived):
    peers, height, _ = arrived.shape
    return pl.pallas_call(
        share_kernel,
        in_specs=[VMEM],
        out_specs=[VMEM, VMEM],
        out_shape=[
            jax.ShapeDtypeStruct((peers, height - 8, LANES), F32),
            jax.ShapeDtypeStruct((8, LANES), F32),
        ],
        compiler_params=SMALL,
        name="share",
    )(arrived)


def factor_kernel(rows_total, gram_ref, sketch_ref, inverse_ref, basis_ref):
    rank = sketch_ref.shape[0]
    inverse = inverse_factor(unpacked(gram_ref[...], rank) * (1.0 / rows_total))
    inverse_ref[...] = inverse
    basis_ref[...] = jnp.dot(
        inverse, sketch_ref[...], precision=HIGHEST, preferred_element_type=F32
    )


def factor_call(gram, sketch, rows_total):
    rank = sketch.shape[0]
    return pl.pallas_call(
        functools.partial(factor_kernel, rows_total),
        in_specs=[VMEM, VMEM],
        out_specs=[VMEM, VMEM],
        out_shape=[
            jax.ShapeDtypeStruct((rank, rank), F32),
            jax.ShapeDtypeStruct(sketch.shape, F32),
        ],
        compiler_params=SMALL,
        cost_estimate=pl.CostEstimate(
            flops=1 << 30, bytes_accessed=8 << 20, transcendentals=0
        ),
        name="factor",
    )(gram, sketch)


def core_kernel(order, arrived_ref, inverse_ref, core_ref):
    square = restored(jnp.sum(arrived_ref[...], axis=0), core_ref.shape[0]) * (1.0 / order)
    inverse = inverse_ref[...]
    half = jnp.dot(inverse, square, precision=HIGHEST, preferred_element_type=F32)
    core_ref[...] = lax.dot_general(
        half, inverse, NT, precision=HIGHEST, preferred_element_type=F32
    )


def core_call(arrived, inverse, order):
    return pl.pallas_call(
        functools.partial(core_kernel, order),
        in_specs=[VMEM, VMEM],
        out_specs=VMEM,
        out_shape=jax.ShapeDtypeStruct(inverse.shape, F32),
        compiler_params=SMALL,
        name="core",
    )(arrived, inverse)


def square_kernel(arrived_ref, square_ref):
    senders, height, _ = arrived_ref.shape
    rank = height // 2
    pieces = [
        arrived_ref[sender, piece * rank : (piece + 1) * rank, :]
        for sender in range(senders)
        for piece in range(2)
    ]
    image = jnp.concatenate(pieces, 1)
    flat = flattened(
        lax.dot_general(image, image, NT, precision=HIGHEST, preferred_element_type=F32)
    )
    for copy in range(square_ref.shape[0]):
        square_ref[copy] = flat


def square_call(arrived, copies):
    rank = arrived.shape[1] // 2
    return pl.pallas_call(
        square_kernel,
        in_specs=[VMEM],
        out_specs=VMEM,
        out_shape=jax.ShapeDtypeStruct((copies, rank * rank // LANES, LANES), F32),
        compiler_params=SMALL,
        name="square",
    )(arrived)


def joined_kernel(own_ref, other_ref, inverse_ref, image_ref, same_ref):
    same_ref[...] = inverse_ref[...]
    core = lax.axis_index("c")
    rank = image_ref.shape[0]
    senders, height, _ = own_ref.shape
    pieces = height // rank
    span = pieces * LANES
    for ref, half in ((own_ref, core), (other_ref, 1 - core)):
        raw = jnp.concatenate(
            [
                ref[sender, piece * rank : (piece + 1) * rank, :]
                for sender in range(senders)
                for piece in range(pieces)
            ],
            1,
        )
        image = jnp.dot(
            inverse_ref[...], raw, precision=HIGHEST, preferred_element_type=F32
        )
        for sender in range(senders):
            at = pl.multiple_of((2 * sender + half) * span, LANES)
            image_ref[:, pl.ds(at, span)] = image[:, sender * span : (sender + 1) * span]


def joined_call(own, other, inverse):
    senders, height, _ = own.shape
    rank = inverse.shape[0]
    return pl.pallas_call(
        joined_kernel,
        in_specs=[VMEM, VMEM, VMEM],
        out_specs=[VMEM, VMEM],
        out_shape=[
            jax.ShapeDtypeStruct((rank, 2 * senders * height // rank * LANES), F32),
            jax.ShapeDtypeStruct(inverse.shape, F32),
        ],
        compiler_params=SMALL,
        name="joined",
    )(own, other, inverse)


def shards(row_cells, col_cells, omega):
    rank = omega.shape[0]
    local_rows = row_cells.shape[1]
    local_cols = col_cells.shape[1]
    rows_total = local_rows * lax.axis_size(ROW)
    order = local_cols * lax.axis_size(COL)
    peers = lax.axis_size("x")
    parts, matrix = sketch_call(row_cells, col_cells, omega, peers, lax.axis_size(ROW), 4)
    over_x = resend_call(exchanged(parts, "x"), lax.axis_size("zh"), "over_x")
    over_both = resend_call(exchanged(over_x, "zh"), peers, "over_zh")
    first, second, sketch = image_calls(exchanged(over_both, "x"), matrix, 2)
    chip_parts = pair_call(second, swapped(first))
    shares, gram = share_call(exchanged(chip_parts, ("zl", "y")))
    own = exchanged(shares, ("zl", "y"))
    inverse, basis = factor_call(gram, sketch, rows_total)
    square_parts = square_call(own, lax.axis_size(COL + ("c",)))
    own, square_parts = lax.optimization_barrier((own, square_parts))
    image, inverse = joined_call(own, swapped(own), inverse)
    core = core_call(exchanged(square_parts, COL + ("c",)), inverse, order)
    return (basis, image, core)


def solution(mesh):
    finer = Mesh(mesh.devices.reshape(4, 4, 2, 4, 4), ROW + COL)
    return jax.shard_map(
        shards,
        mesh=finer,
        in_specs=(P(None, ROW), P(None, COL), P(None, COL)),
        out_specs=(P(None, ROW), P(None, COL), P()),
        check_vma=False,
    )
```
